32 devices in a mesh: gx: 16 (over z, y, x), bl: 2 (over core).
Axes of the slice: x: 2, y: 2, z: 4, core: 2. Of those that a mesh axis runs over, the one named last changes fastest.
Arguments:
- voltages: bfloat16 [2, 1024, 71680], P('bl', 'gx'), may hold values from -10 to 10, as said below
- model_magnitude: float32 [16, 2048], P('gx'), may hold values from 0.06 to 0.25
- model_phase: float32 [16, 2048], P('gx'), may hold values from -3.140625 to 3.140625
Outputs:
- visibilities: bfloat16 [16, 2, 2048, 2048], P('gx', None, 'bl')
- gains: float32 [2, 2, 1024, 16], P(None, 'bl', 'gx')
The draws below stay inside these ranges and needn't reach their ends.
Inputs may be any that keep to these rules, and one draw needn't show every extreme that they name: `voltages`: each input's sampled voltage stream.
All inputs are finite; a program needn't handle non-finite values.
Results may differ from the reference program's by a relative error of at most 0.0057.
Values may be sent and summed in bfloat16 or wider, within the bound.
A program may use at most 64 MiB of HBM per device.

```python
import math
import jax
import jax.numpy as jnp
from jax import lax

INPUTS = 2048
NFFT = 2048
TAPS = 4
SPECTRA = 32
ITERS = 4
CHANNELS = 16
TILES = 2
HALF = 1024
SAMPLES = 71680
STRIDE = 64


def draw_voltages(key, part):
    key_strength = jax.random.fold_in(jax.random.fold_in(key, 17), 0)
    key_source = jax.random.fold_in(jax.random.fold_in(key, 17), 1)
    key_noise = jax.random.fold_in(jax.random.fold_in(key, 17), 3)
    strength = jnp.exp(jax.random.uniform(key_strength, (TILES, HALF, 1), jnp.float32, math.log(0.12), math.log(0.4)))
    source = jax.random.truncated_normal(key_source, -4.0, 4.0, (1, 1, SAMPLES), jnp.float32)
    noise_part = 2.0 * jax.random.truncated_normal(key_noise, -4.0, 4.0, (TILES, HALF, SAMPLES), jnp.float32)
    return (noise_part + strength * source).astype(jnp.bfloat16)


def level_of(own_key, shape, shards, low, high):
    factor_of = 1.0
    for axis_at, parts in shards:
        draws = jax.random.uniform(jax.random.fold_in(jax.random.fold_in(own_key, 6), axis_at), (parts,), jnp.float32, low / len(shards), high / len(shards))
        factor_of = factor_of * jnp.repeat(jnp.exp(draws), shape[axis_at] // parts).reshape((-1,) + (1,) * (len(shape) - 1 - axis_at))
    return factor_of


def setup_inputs(seed: int = 0) -> dict:
    key_list = jax.random.split(jax.random.key(seed), 4)
    return {
        "voltages": draw_voltages(jax.random.fold_in(key_list[3], 71), 0),
        "model_magnitude": jnp.clip(jnp.exp(math.log(0.25) - 1.4271164 * jax.random.uniform(key_list[1], (CHANNELS, INPUTS), jnp.float32) ** level_of(key_list[1], (CHANNELS, INPUTS), ((0, 16),), -0.2, 0.2)), 0.06, 0.25),
        "model_phase": jnp.clip(jax.random.uniform(key_list[2], (CHANNELS, INPUTS), jnp.float32, -3.140625, 3.140625), -3.140625, 3.140625),
    }


def window_table(tap_count, length):
    positions = jnp.arange(tap_count * length, dtype=jnp.float32)
    centre = (positions + 0.5) / length - tap_count / 2.0
    hann_taper = 0.5 - 0.5 * jnp.cos(2.0 * math.pi * (positions + 0.5) / (tap_count * length))
    return (jnp.sinc(centre) * hann_taper).reshape(tap_count, length)

def reference(voltages, model_magnitude, model_phase):
    frames_total = SPECTRA + TAPS - 1
    taps_window = window_table(TAPS, NFFT)
    bin_index = (jnp.arange(CHANNELS, dtype=jnp.int32) * STRIDE + (STRIDE + 1) // 2).astype(jnp.int32)

    def channelize(row_block):
        framed = row_block.reshape(row_block.shape[0], frames_total, NFFT).astype(jnp.float32)
        summed = framed[:, 0:SPECTRA, :] * taps_window[0]
        for tap_index in range(1, TAPS):
            summed = summed + framed[:, tap_index:tap_index + SPECTRA, :] * taps_window[tap_index]
        spectrum = jnp.fft.rfft(summed, axis=2)
        picked = jnp.take(spectrum, bin_index, axis=2)
        real_part = (jnp.real(picked) / math.sqrt(NFFT)).astype(jnp.float32)
        imag_part = (jnp.imag(picked) / math.sqrt(NFFT)).astype(jnp.float32)
        return jnp.stack([real_part, imag_part], axis=0).astype(jnp.bfloat16)
    row_blocks = voltages.reshape(INPUTS // 64, 64, SAMPLES)
    channelized = lax.map(channelize, row_blocks)
    spectra_all = jnp.transpose(channelized, (4, 1, 0, 2, 3)).reshape(CHANNELS, 2, INPUTS, SPECTRA)
    identity = jnp.arange(INPUTS)[:, None] == jnp.arange(INPUTS)[None, :]

    def per_channel(packed):
        spectra_one, magnitude, phase_row = packed
        dense_values = spectra_one.astype(jnp.float32)
        left_side = jnp.concatenate([dense_values[0], dense_values[1]], axis=1)
        lower_side = jnp.concatenate([dense_values[1], -dense_values[0]], axis=1)
        real_power = jnp.dot(left_side, left_side.T, precision=lax.Precision.HIGHEST) * (1.0 / SPECTRA)
        imag_power = jnp.dot(lower_side, left_side.T, precision=lax.Precision.HIGHEST) * (1.0 / SPECTRA)
        hollow_real = jnp.where(identity, jnp.float32(0.0), real_power)
        hollow_imag = jnp.where(identity, jnp.float32(0.0), imag_power)
        model_real = magnitude * jnp.cos(phase_row)
        model_imag = magnitude * jnp.sin(phase_row)
        inverse_square = 1.0 / (magnitude * magnitude)
        gain_real = jnp.ones((INPUTS,), jnp.float32)
        gain_imag = jnp.zeros((INPUTS,), jnp.float32)
        for step_index in range(ITERS):
            probe_real = gain_real * model_real - gain_imag * model_imag
            probe_imag = gain_real * model_imag + gain_imag * model_real
            image_real = jnp.dot(hollow_real, probe_real, precision=lax.Precision.HIGHEST) - jnp.dot(hollow_imag, probe_imag, precision=lax.Precision.HIGHEST)
            image_imag = jnp.dot(hollow_real, probe_imag, precision=lax.Precision.HIGHEST) + jnp.dot(hollow_imag, probe_real, precision=lax.Precision.HIGHEST)
            energy = jnp.sum(probe_real * probe_real + probe_imag * probe_imag) + 1e-06
            factor = inverse_square / energy
            fresh_real = (image_real * model_real + image_imag * model_imag) * factor
            fresh_imag = (image_imag * model_real - image_real * model_imag) * factor
            if step_index % 2 == 1:
                gain_real = (fresh_real + gain_real) * 0.5
                gain_imag = (fresh_imag + gain_imag) * 0.5
            else:
                gain_real = fresh_real
                gain_imag = fresh_imag
        visible = jnp.stack([real_power, imag_power], axis=0).astype(jnp.bfloat16)
        return (visible, jnp.stack([gain_real, gain_imag], axis=0))
    visibilities, gain_table = lax.map(per_channel, (spectra_all, model_magnitude, model_phase))
    gains = jnp.transpose(gain_table, (1, 2, 0)).reshape(2, TILES, HALF, CHANNELS)
    return (visibilities, gains)
```

```python
import math

import jax
import jax.numpy as jnp
import numpy as np
from jax import lax
from jax.experimental import pallas as pl
from jax.experimental.pallas import tpu as pltpu
from jax.sharding import PartitionSpec as P

NFFT = 2048
TAPS = 4
ITERS = 4
LANES = 128


epsilon = 1e-06


def window_table(tap_count, length):
    positions = jnp.arange(tap_count * length, dtype=jnp.float32)
    centre = (positions + 0.5) / length - tap_count / 2.0
    hann_taper = 0.5 - 0.5 * jnp.cos(2.0 * math.pi * (positions + 0.5) / (tap_count * length))
    return (jnp.sinc(centre) * hann_taper).reshape(tap_count, length)


def channel_table(channels, stride, length):
    bin_index = jnp.arange(channels, dtype=jnp.int32) * stride + (stride + 1) // 2
    sample_index = jnp.arange(length, dtype=jnp.int32)
    phase_index = bin_index[:, None] * sample_index[None, :] % length
    angles = phase_index.astype(jnp.float32) * (2.0 * math.pi / length)
    factor = 1.0 / math.sqrt(length)
    return jnp.stack([jnp.cos(angles) * factor, -jnp.sin(angles) * factor], axis=1)


def stack_left(row_block):
    real_part = row_block[:, 0]
    imag_part = row_block[:, 1]
    upper = jnp.concatenate([real_part, imag_part], axis=2)
    lower = jnp.concatenate([imag_part, -real_part], axis=2)
    return jnp.stack([upper, lower], axis=1)


def on_device(voltages, model_magnitude, model_phase):
    groups = lax.axis_size("gx")
    local_channels = model_magnitude.shape[0]
    channels = local_channels * groups
    inputs = model_magnitude.shape[1]
    half_rows = inputs // lax.axis_size("bl")
    owned_inputs = voltages.shape[1]
    frames_total = voltages.shape[2] // NFFT
    spectra = frames_total - TAPS + 1
    taps_window = window_table(TAPS, NFFT)
    blocks = voltages.reshape(owned_inputs, frames_total, NFFT)
    frames = blocks[:, 0:spectra, :].astype(jnp.float32) * taps_window[0]
    for tap_index in range(1, TAPS):
        frames = (
            frames
            + blocks[:, tap_index : tap_index + spectra, :].astype(jnp.float32)
            * taps_window[tap_index]
        )
    stride = NFFT // 2 // channels
    transform = channel_table(channels, stride, NFFT).reshape(2 * channels, NFFT)
    spectra_local = lax.dot_general(
        transform,
        frames.reshape(owned_inputs * spectra, NFFT),
        (((1,), (1,)), ((), ())),
        precision=lax.Precision.HIGHEST,
        preferred_element_type=jnp.float32,
    )
    spectra_local = spectra_local.reshape(channels, 2, owned_inputs, spectra).astype(jnp.bfloat16)
    tile_index = lax.axis_index("bl")
    row_start = tile_index * half_rows
    own_rows = lax.all_to_all(spectra_local, "gx", split_axis=0, concat_axis=2, tiled=True)
    left_side = stack_left(own_rows)
    portion = lax.all_gather(own_rows, "bl", axis=2, tiled=True)
    right_side = jnp.concatenate([portion[:, 0], portion[:, 1]], axis=2)
    block_power = jnp.einsum(
        "cohk,crk->cohr", left_side, right_side, preferred_element_type=jnp.float32
    )
    whole_inputs = portion
    cross_sum, whole_inputs = (block_power, whole_inputs)
    cross_power = cross_sum * (1.0 / spectra)
    model_real = model_magnitude * jnp.cos(model_phase)
    model_imag = model_magnitude * jnp.sin(model_phase)
    inverse_square = 1.0 / (model_magnitude * model_magnitude)
    highest = lax.Precision.HIGHEST
    dense_values = whole_inputs.astype(jnp.float32)
    diagonal = jnp.sum(dense_values * dense_values, axis=(1, 3)) * (1.0 / spectra)

    def apply_power(probe_real, probe_imag):
        inner_real = jnp.einsum(
            "cps,cp->cs", dense_values[:, 0], probe_real, precision=highest
        ) + jnp.einsum("cps,cp->cs", dense_values[:, 1], probe_imag, precision=highest)
        inner_imag = jnp.einsum(
            "cps,cp->cs", dense_values[:, 0], probe_imag, precision=highest
        ) - jnp.einsum("cps,cp->cs", dense_values[:, 1], probe_real, precision=highest)
        real_out = (
            jnp.einsum("cps,cs->cp", dense_values[:, 0], inner_real, precision=highest)
            - jnp.einsum("cps,cs->cp", dense_values[:, 1], inner_imag, precision=highest)
        ) * (1.0 / spectra) - diagonal * probe_real
        imag_out = (
            jnp.einsum("cps,cs->cp", dense_values[:, 0], inner_imag, precision=highest)
            + jnp.einsum("cps,cs->cp", dense_values[:, 1], inner_real, precision=highest)
        ) * (1.0 / spectra) - diagonal * probe_imag
        return (real_out, imag_out)

    def single_step(gain_real, gain_imag):
        probe_real = gain_real * model_real - gain_imag * model_imag
        probe_imag = gain_real * model_imag + gain_imag * model_real
        image_real, image_imag = apply_power(probe_real, probe_imag)
        energy = (
            jnp.sum(probe_real * probe_real + probe_imag * probe_imag, axis=1, keepdims=True)
            + epsilon
        )
        factor = inverse_square / energy
        fresh_real = (image_real * model_real + image_imag * model_imag) * factor
        fresh_imag = (image_imag * model_real - image_real * model_imag) * factor
        return (fresh_real, fresh_imag)

    def double_step(pair_index, current):
        first_real, first_imag = single_step(current[0], current[1])
        fresh_real, fresh_imag = single_step(first_real, first_imag)
        return ((fresh_real + first_real) * 0.5, (fresh_imag + first_imag) * 0.5)

    start_gains = (
        jnp.ones((local_channels, inputs), jnp.float32),
        jnp.zeros((local_channels, inputs), jnp.float32),
    )
    gain_real, gain_imag = lax.fori_loop(0, ITERS // 2, double_step, start_gains)
    gain_pair = jnp.stack([gain_real, gain_imag], axis=1)
    own_gains = lax.dynamic_slice_in_dim(gain_pair, row_start, half_rows, 2)
    everything = lax.all_gather(own_gains, "gx", axis=0, tiled=True)
    owned_start = lax.axis_index("gx") * owned_inputs
    owned_gains = lax.dynamic_slice_in_dim(everything, owned_start, owned_inputs, 2)
    gain_output = jnp.transpose(owned_gains, (1, 2, 0))[:, None]
    return (cross_power.astype(jnp.bfloat16), gain_output)


def filter_bank(channels, stride):
    position = (np.arange(TAPS * NFFT) + 0.5).reshape(TAPS, NFFT)
    taper = np.sinc(position / NFFT - TAPS / 2.0) * (
        0.5 - 0.5 * np.cos(2.0 * math.pi * position / (TAPS * NFFT))
    )
    bins = np.arange(channels) * stride + (stride + 1) // 2
    angle = (bins[:, None] * np.arange(NFFT)[None, :] % NFFT) * (2.0 * math.pi / NFFT)
    waves = np.stack([np.cos(angle), -np.sin(angle)]) / math.sqrt(NFFT)
    bank = (taper[:, None, None, :] * waves[None]).reshape(TAPS * 2 * channels, NFFT)
    high = bank.astype(jnp.bfloat16)
    low = (bank - high.astype(np.float64)).astype(jnp.bfloat16)
    return np.concatenate([high, low], axis=0)


def channelize(v_ref, bank_ref, mag_ref, phase_ref, msg_ref, mr_ref, mi_ref, y_ref, f_ref):
    step = pl.program_id(0)
    owned = v_ref.shape[1]
    per_step = v_ref.shape[2] // NFFT
    channels, _, pairs, _ = msg_ref.shape
    rows = jnp.concatenate(
        [v_ref[0, :, k * NFFT : (k + 1) * NFFT] for k in range(per_step)], axis=0
    )
    y = lax.dot_general(
        bank_ref[...], rows, (((1,), (1,)), ((), ())), preferred_element_type=jnp.float32
    )
    half = y.shape[0] // 2
    y = y[:half] + y[half:]
    tiles = y.shape[1] // LANES
    for k in range(tiles):
        y_ref[step * tiles + k] = y[:, k * LANES : (k + 1) * LANES]

    @pl.when(step == 0)
    def _():
        mr_ref[...] = mag_ref[...] * jnp.cos(phase_ref[...])
        mi_ref[...] = mag_ref[...] * jnp.sin(phase_ref[...])

    @pl.when(step == pl.num_programs(0) - 1)
    def _():
        group = 2 * channels
        low = lax.broadcasted_iota(jnp.int32, (group, LANES), 1) < owned

        def part(tap, tile):
            return y_ref[tile, tap * group : (tap + 1) * group, :]

        turned = pltpu.roll(part(1, 0) + part(3, 1), owned, 1)
        for j in range(pairs):
            following = pltpu.roll(part(1, j + 1) + part(3, j + 2), owned, 1)
            total = part(0, j) + part(2, j + 1) + jnp.where(low, turned, following)
            f_ref[pl.ds(j, group, stride=pairs), :] = total
            turned = following
        for r in range(2):
            for c in range(channels):
                start = (r * channels + c) * pairs
                msg_ref[c, r] = f_ref[start : start + pairs, :].astype(jnp.bfloat16)


def exchange(
    msg_ref, mag_ref, mr_ref, mi_ref, right_ref, own_ref, gain_ref,
    slots, dense, yr_ref, yi_ref, wr_ref, wi_ref, gr_ref, gi_ref, pack, landed,
    send_sem, recv_sem, fsend_sem, frecv_sem, gsend_sem, grecv_sem, local_sem,
):
    groups = lax.axis_size("gx")
    g = lax.axis_index("gx")
    b = lax.axis_index("bl")
    other = 1 - b
    mesh_id = pl.DeviceIdType.MESH
    pairs = msg_ref.shape[2]
    spectra = 2 * pairs
    tiles = dense.shape[0]
    owned = LANES // 2

    barrier = pltpu.get_barrier_semaphore()

    def greet(k, carry):
        pl.semaphore_signal(
            barrier, inc=1, device_id=(lax.rem(g + k, groups), b), device_id_type=mesh_id
        )
        return carry

    lax.fori_loop(1, groups, greet, 0)
    pl.semaphore_signal(barrier, inc=1, device_id=(g, other), device_id_type=mesh_id)
    pl.semaphore_wait(barrier, groups)

    def spread(k, source):
        peer = lax.rem(g + k, groups)
        return pltpu.make_async_remote_copy(
            src_ref=msg_ref.at[peer], dst_ref=slots.at[b, source],
            send_sem=send_sem.at[k], recv_sem=recv_sem.at[k],
            device_id=(peer, b), device_id_type=mesh_id,
        )

    def relay(k, side):
        source = lax.rem(g + groups - k, groups)
        return pltpu.make_async_remote_copy(
            src_ref=slots.at[b, source], dst_ref=slots.at[side, source],
            send_sem=fsend_sem.at[k], recv_sem=frecv_sem.at[k],
            device_id=(g, other), device_id_type=mesh_id,
        )

    def start_spread(k, carry):
        spread(k, g).start()
        return carry

    lax.fori_loop(1, groups, start_spread, 0)
    mine = pltpu.make_async_copy(msg_ref.at[g], slots.at[b, g], local_sem)
    mine.start()
    mine.wait()
    relay(0, b).start()

    def pass_on(k, carry):
        spread(k, lax.rem(g + groups - k, groups)).wait_recv()
        relay(k, b).start()
        return carry

    lax.fori_loop(1, groups, pass_on, 0)

    def collect(k, carry):
        relay(k, other).wait_recv()
        return carry

    lax.fori_loop(0, groups, collect, 0)

    low = lax.broadcasted_iota(jnp.int32, (pairs, LANES), 1) < owned
    for side in range(2):
        for t in range(groups // 2):
            tile = side * (groups // 2) + t
            for r in range(2):
                first = slots[side, 2 * t, r].astype(jnp.float32)
                second = slots[side, 2 * t + 1, r].astype(jnp.float32)
                even = jnp.where(low, first, pltpu.roll(second, owned, 1))
                odd = jnp.where(low, pltpu.roll(first, owned, 1), second)
                both = jnp.concatenate([even, odd], axis=0)
                dense[tile, r * spectra : (r + 1) * spectra, :] = both
                right_ref[
                    r * spectra : (r + 1) * spectra, tile * LANES : (tile + 1) * LANES
                ] = both.astype(jnp.bfloat16)
            diagonal = jnp.sum(dense[tile] * dense[tile], axis=0, keepdims=True)
            wr_ref[tile : tile + 1, :] = diagonal
    for t in range(groups // 2):
        own_ref[t] = dense[b * (groups // 2) + t]

    scale = 1.0 / spectra
    diagonal = wr_ref[...] * scale
    model_real = mr_ref[...]
    model_imag = mi_ref[...]
    magnitude = mag_ref[...]
    inverse_square = 1.0 / (magnitude * magnitude)

    def single_step(gain_real, gain_imag):
        probe_real = gain_real * model_real - gain_imag * model_imag
        probe_imag = gain_real * model_imag + gain_imag * model_real
        yr_ref[...] = probe_real
        yi_ref[...] = probe_imag
        total_real = jnp.zeros((spectra, LANES), jnp.float32)
        total_imag = jnp.zeros((spectra, LANES), jnp.float32)
        for t in range(tiles):
            re = dense[t, :spectra, :]
            im = dense[t, spectra:, :]
            yr = yr_ref[t : t + 1, :]
            yi = yi_ref[t : t + 1, :]
            total_real = total_real + (re * yr + im * yi)
            total_imag = total_imag + (re * yi - im * yr)
        inner_real = jnp.sum(total_real, axis=1, keepdims=True) * scale
        inner_imag = jnp.sum(total_imag, axis=1, keepdims=True) * scale
        inner_real = jnp.broadcast_to(inner_real, (spectra, LANES))
        inner_imag = jnp.broadcast_to(inner_imag, (spectra, LANES))
        for t in range(tiles):
            re = dense[t, :spectra, :]
            im = dense[t, spectra:, :]
            wr_ref[t : t + 1, :] = jnp.sum(
                re * inner_real - im * inner_imag, axis=0, keepdims=True
            )
            wi_ref[t : t + 1, :] = jnp.sum(
                re * inner_imag + im * inner_real, axis=0, keepdims=True
            )
        image_real = wr_ref[...] - diagonal * probe_real
        image_imag = wi_ref[...] - diagonal * probe_imag
        energy = jnp.sum(
            jnp.sum(probe_real * probe_real + probe_imag * probe_imag, axis=1, keepdims=True),
            axis=0,
            keepdims=True,
        ) + epsilon
        factor = inverse_square / energy
        fresh_real = (image_real * model_real + image_imag * model_imag) * factor
        fresh_imag = (image_imag * model_real - image_real * model_imag) * factor
        return (fresh_real, fresh_imag)

    def double_step(pair_index, current):
        first_real, first_imag = single_step(current[0], current[1])
        fresh_real, fresh_imag = single_step(first_real, first_imag)
        return ((fresh_real + first_real) * 0.5, (fresh_imag + first_imag) * 0.5)

    gain_real, gain_imag = lax.fori_loop(
        0,
        ITERS // 2,
        double_step,
        (jnp.ones((tiles, LANES), jnp.float32), jnp.zeros((tiles, LANES), jnp.float32)),
    )
    gr_ref[...] = gain_real
    gi_ref[...] = gain_imag
    half = groups // 2
    own_real = gr_ref[pl.ds(pl.multiple_of(b * half, half), half), :]
    own_imag = gi_ref[pl.ds(pl.multiple_of(b * half, half), half), :]
    low = lax.broadcasted_iota(jnp.int32, (half, LANES), 1) < owned
    even = jnp.where(low, own_real, pltpu.roll(own_imag, owned, 1))
    odd = jnp.where(low, pltpu.roll(own_real, owned, 1), own_imag)
    for t in range(half):
        pack[2 * t] = even[t : t + 1, :]
        pack[2 * t + 1] = odd[t : t + 1, :]

    def hand_back(k, owner):
        peer = lax.rem(g + k, groups)
        return pltpu.make_async_remote_copy(
            src_ref=pack.at[peer], dst_ref=landed.at[owner],
            send_sem=gsend_sem.at[k], recv_sem=grecv_sem.at[k],
            device_id=(peer, b), device_id_type=mesh_id,
        )

    def start_back(k, carry):
        hand_back(k, g).start()
        return carry

    lax.fori_loop(1, groups, start_back, 0)
    landed[g] = pack[g]

    def drain(k, carry):
        spread(k, g).wait_send()
        relay(k, b).wait_send()
        hand_back(k, g).wait_send()
        hand_back(k, lax.rem(g + groups - k, groups)).wait_recv()
        return carry

    relay(0, b).wait_send()
    lax.fori_loop(1, groups, drain, 0)
    for c in range(groups):
        gain_ref[c : c + 1, :] = landed[c]


def correlate(own_ref, right_ref, out_ref, real_side, imag_side):
    depth = right_ref.shape[0]
    spectra = depth // 2

    @pl.when(pl.program_id(0) == 0)
    def _():
        real_side[:depth, :] = right_ref[...]
        real_side[depth:, :] = jnp.zeros_like(right_ref)
        imag_side[:depth, :] = jnp.zeros_like(right_ref)
        imag_side[depth:, :] = right_ref[...]

    own = own_ref[0] * (1.0 / spectra)
    left = jnp.concatenate([own, own[spectra:], -own[:spectra]], axis=0)
    left = jnp.transpose(left).astype(jnp.bfloat16)
    out_ref[0, 0] = jnp.dot(
        left, real_side[...], preferred_element_type=jnp.float32
    ).astype(jnp.bfloat16)
    out_ref[0, 1] = jnp.dot(
        left, imag_side[...], preferred_element_type=jnp.float32
    ).astype(jnp.bfloat16)


def on_device_tiled(voltages, model_magnitude, model_phase):
    groups = lax.axis_size("gx")
    inputs = model_magnitude.shape[1]
    owned = voltages.shape[1]
    frames_total = voltages.shape[2] // NFFT
    spectra = frames_total - TAPS + 1
    pairs = spectra // 2
    per_step = 2 * LANES // owned
    steps = -(-frames_total // per_step)
    tiles = inputs // LANES
    half = tiles // 2
    bank = jnp.asarray(filter_bank(groups, NFFT // 2 // groups))
    magnitude = model_magnitude.reshape(tiles, LANES)
    phase = model_phase.reshape(tiles, LANES)
    f32 = jnp.float32
    whole = lambda i: (0, 0)
    table = jax.ShapeDtypeStruct((tiles, LANES), f32)
    table_spec = pl.BlockSpec((tiles, LANES), whole)
    messages, model_real, model_imag = pl.pallas_call(
        channelize,
        grid=(steps,),
        in_specs=[
            pl.BlockSpec((1, owned, per_step * NFFT), lambda i: (0, 0, i)),
            pl.BlockSpec(bank.shape, whole),
            table_spec,
            table_spec,
        ],
        out_specs=[
            pl.BlockSpec((groups, 2, pairs, LANES), lambda i: (0, 0, 0, 0)),
            table_spec,
            table_spec,
        ],
        out_shape=[
            jax.ShapeDtypeStruct((groups, 2, pairs, LANES), jnp.bfloat16),
            table,
            table,
        ],
        scratch_shapes=[
            pltpu.VMEM((steps * 2, TAPS * 2 * groups, LANES), f32),
            pltpu.VMEM((2 * groups * pairs, LANES), f32),
        ],
        compiler_params=pltpu.CompilerParams(dimension_semantics=("arbitrary",)),
        name="channelize",
    )(voltages, bank, magnitude, phase)
    vmem = pl.BlockSpec(memory_space=pltpu.VMEM)
    right, own, gains = pl.pallas_call(
        exchange,
        in_specs=[vmem] * 4,
        out_specs=[vmem] * 3,
        out_shape=[
            jax.ShapeDtypeStruct((2 * spectra, inputs), jnp.bfloat16),
            jax.ShapeDtypeStruct((half, 2 * spectra, LANES), f32),
            jax.ShapeDtypeStruct((groups, LANES), f32),
        ],
        scratch_shapes=[
            pltpu.VMEM((2, groups, 2, pairs, LANES), jnp.bfloat16),
            pltpu.VMEM((tiles, 2 * spectra, LANES), f32),
        ]
        + [pltpu.VMEM((tiles, LANES), f32)] * 6
        + [pltpu.VMEM((groups, 1, LANES), f32)] * 2
        + [pltpu.SemaphoreType.DMA((groups,))] * 6
        + [pltpu.SemaphoreType.DMA],
        compiler_params=pltpu.CompilerParams(collective_id=0, has_side_effects=True),
        name="exchange",
    )(messages, magnitude, model_real, model_imag)
    visibilities = pl.pallas_call(
        correlate,
        grid=(half,),
        in_specs=[
            pl.BlockSpec((1, 2 * spectra, LANES), lambda i: (i, 0, 0)),
            pl.BlockSpec((2 * spectra, inputs), whole),
        ],
        out_specs=pl.BlockSpec((1, 2, LANES, inputs), lambda i: (0, 0, i, 0)),
        out_shape=jax.ShapeDtypeStruct((1, 2, half * LANES, inputs), jnp.bfloat16),
        scratch_shapes=[pltpu.VMEM((4 * spectra, inputs), jnp.bfloat16)] * 2,
        compiler_params=pltpu.CompilerParams(dimension_semantics=("arbitrary",)),
        name="correlate",
    )(own, right)
    gains = jnp.transpose(gains.reshape(groups, 2, owned), (1, 2, 0))[:, None]
    return (visibilities, gains)


def solution(mesh):
    in_specs = (P("bl", "gx", None), P("gx", None), P("gx", None))
    out_specs = (P("gx", None, "bl", None), P(None, "bl", "gx", None))

    def body(voltages, model_magnitude, model_phase):
        spectra = voltages.shape[2] // NFFT - TAPS + 1
        groups = mesh.shape["gx"]
        tiled = (
            model_magnitude.shape[0] == 1
            and 2 * voltages.shape[1] == LANES
            and mesh.shape["bl"] == 2
            and groups % 16 == 0
            and spectra % 32 == 0
            and spectra & (spectra - 1) == 0
        )
        run = on_device_tiled if tiled else on_device
        return run(voltages, model_magnitude, model_phase)

    return jax.shard_map(
        body, mesh=mesh, in_specs=in_specs, out_specs=out_specs, check_vma=False
    )
```

```python
import math

import jax
import jax.numpy as jnp
import numpy as np
from jax import lax
from jax.experimental import pallas as pl
from jax.experimental.pallas import tpu as pltpu
from jax.sharding import PartitionSpec as P

NFFT = 2048
TAPS = 4
ITERS = 4
LANES = 128


epsilon = 1e-06


def window_table(tap_count, length):
    positions = jnp.arange(tap_count * length, dtype=jnp.float32)
    centre = (positions + 0.5) / length - tap_count / 2.0
    hann_taper = 0.5 - 0.5 * jnp.cos(2.0 * math.pi * (positions + 0.5) / (tap_count * length))
    return (jnp.sinc(centre) * hann_taper).reshape(tap_count, length)


def channel_table(channels, stride, length):
    bin_index = jnp.arange(channels, dtype=jnp.int32) * stride + (stride + 1) // 2
    sample_index = jnp.arange(length, dtype=jnp.int32)
    phase_index = bin_index[:, None] * sample_index[None, :] % length
    angles = phase_index.astype(jnp.float32) * (2.0 * math.pi / length)
    factor = 1.0 / math.sqrt(length)
    return jnp.stack([jnp.cos(angles) * factor, -jnp.sin(angles) * factor], axis=1)


def stack_left(row_block):
    real_part = row_block[:, 0]
    imag_part = row_block[:, 1]
    upper = jnp.concatenate([real_part, imag_part], axis=2)
    lower = jnp.concatenate([imag_part, -real_part], axis=2)
    return jnp.stack([upper, lower], axis=1)


def on_device(voltages, model_magnitude, model_phase):
    groups = lax.axis_size("gx")
    local_channels = model_magnitude.shape[0]
    channels = local_channels * groups
    inputs = model_magnitude.shape[1]
    half_rows = inputs // lax.axis_size("bl")
    owned_inputs = voltages.shape[1]
    frames_total = voltages.shape[2] // NFFT
    spectra = frames_total - TAPS + 1
    taps_window = window_table(TAPS, NFFT)
    blocks = voltages.reshape(owned_inputs, frames_total, NFFT)
    frames = blocks[:, 0:spectra, :].astype(jnp.float32) * taps_window[0]
    for tap_index in range(1, TAPS):
        frames = (
            frames
            + blocks[:, tap_index : tap_index + spectra, :].astype(jnp.float32)
            * taps_window[tap_index]
        )
    stride = NFFT // 2 // channels
    transform = channel_table(channels, stride, NFFT).reshape(2 * channels, NFFT)
    spectra_local = lax.dot_general(
        transform,
        frames.reshape(owned_inputs * spectra, NFFT),
        (((1,), (1,)), ((), ())),
        precision=lax.Precision.HIGHEST,
        preferred_element_type=jnp.float32,
    )
    spectra_local = spectra_local.reshape(channels, 2, owned_inputs, spectra).astype(jnp.bfloat16)
    tile_index = lax.axis_index("bl")
    row_start = tile_index * half_rows
    own_rows = lax.all_to_all(spectra_local, "gx", split_axis=0, concat_axis=2, tiled=True)
    left_side = stack_left(own_rows)
    portion = lax.all_gather(own_rows, "bl", axis=2, tiled=True)
    right_side = jnp.concatenate([portion[:, 0], portion[:, 1]], axis=2)
    block_power = jnp.einsum(
        "cohk,crk->cohr", left_side, right_side, preferred_element_type=jnp.float32
    )
    whole_inputs = portion
    cross_sum, whole_inputs = (block_power, whole_inputs)
    cross_power = cross_sum * (1.0 / spectra)
    model_real = model_magnitude * jnp.cos(model_phase)
    model_imag = model_magnitude * jnp.sin(model_phase)
    inverse_square = 1.0 / (model_magnitude * model_magnitude)
    highest = lax.Precision.HIGHEST
    dense_values = whole_inputs.astype(jnp.float32)
    diagonal = jnp.sum(dense_values * dense_values, axis=(1, 3)) * (1.0 / spectra)

    def apply_power(probe_real, probe_imag):
        inner_real = jnp.einsum(
            "cps,cp->cs", dense_values[:, 0], probe_real, precision=highest
        ) + jnp.einsum("cps,cp->cs", dense_values[:, 1], probe_imag, precision=highest)
        inner_imag = jnp.einsum(
            "cps,cp->cs", dense_values[:, 0], probe_imag, precision=highest
        ) - jnp.einsum("cps,cp->cs", dense_values[:, 1], probe_real, precision=highest)
        real_out = (
            jnp.einsum("cps,cs->cp", dense_values[:, 0], inner_real, precision=highest)
            - jnp.einsum("cps,cs->cp", dense_values[:, 1], inner_imag, precision=highest)
        ) * (1.0 / spectra) - diagonal * probe_real
        imag_out = (
            jnp.einsum("cps,cs->cp", dense_values[:, 0], inner_imag, precision=highest)
            + jnp.einsum("cps,cs->cp", dense_values[:, 1], inner_real, precision=highest)
        ) * (1.0 / spectra) - diagonal * probe_imag
        return (real_out, imag_out)

    def single_step(gain_real, gain_imag):
        probe_real = gain_real * model_real - gain_imag * model_imag
        probe_imag = gain_real * model_imag + gain_imag * model_real
        image_real, image_imag = apply_power(probe_real, probe_imag)
        energy = (
            jnp.sum(probe_real * probe_real + probe_imag * probe_imag, axis=1, keepdims=True)
            + epsilon
        )
        factor = inverse_square / energy
        fresh_real = (image_real * model_real + image_imag * model_imag) * factor
        fresh_imag = (image_imag * model_real - image_real * model_imag) * factor
        return (fresh_real, fresh_imag)

    def double_step(pair_index, current):
        first_real, first_imag = single_step(current[0], current[1])
        fresh_real, fresh_imag = single_step(first_real, first_imag)
        return ((fresh_real + first_real) * 0.5, (fresh_imag + first_imag) * 0.5)

    start_gains = (
        jnp.ones((local_channels, inputs), jnp.float32),
        jnp.zeros((local_channels, inputs), jnp.float32),
    )
    gain_real, gain_imag = lax.fori_loop(0, ITERS // 2, double_step, start_gains)
    gain_pair = jnp.stack([gain_real, gain_imag], axis=1)
    own_gains = lax.dynamic_slice_in_dim(gain_pair, row_start, half_rows, 2)
    everything = lax.all_gather(own_gains, "gx", axis=0, tiled=True)
    owned_start = lax.axis_index("gx") * owned_inputs
    owned_gains = lax.dynamic_slice_in_dim(everything, owned_start, owned_inputs, 2)
    gain_output = jnp.transpose(owned_gains, (1, 2, 0))[:, None]
    return (cross_power.astype(jnp.bfloat16), gain_output)


def filter_bank(channels, stride):
    position = (np.arange(TAPS * NFFT) + 0.5).reshape(TAPS, NFFT)
    taper = np.sinc(position / NFFT - TAPS / 2.0) * (
        0.5 - 0.5 * np.cos(2.0 * math.pi * position / (TAPS * NFFT))
    )
    bins = np.arange(channels) * stride + (stride + 1) // 2
    angle = (bins[:, None] * np.arange(NFFT)[None, :] % NFFT) * (2.0 * math.pi / NFFT)
    waves = np.stack([np.cos(angle), -np.sin(angle)]) / math.sqrt(NFFT)
    bank = (taper[:, None, None, :] * waves[None]).reshape(TAPS * 2 * channels, NFFT)
    high = bank.astype(jnp.bfloat16)
    low = (bank - high.astype(np.float64)).astype(jnp.bfloat16)
    return np.concatenate([high, low], axis=0).T


def channelize(v_ref, bank_ref, mag_ref, phase_ref, msg_ref, mr_ref, mi_ref, y_ref, f_ref):
    step = pl.program_id(0)
    owned = v_ref.shape[1]
    per_step = v_ref.shape[2] // NFFT
    channels, _, pairs, _ = msg_ref.shape
    rows = jnp.concatenate(
        [v_ref[0, :, k * NFFT : (k + 1) * NFFT] for k in range(per_step)], axis=0
    )
    y = jnp.dot(rows, bank_ref[...], preferred_element_type=jnp.float32)
    half = y.shape[1] // 2
    y = y[:, :half] + y[:, half:]
    tiles = y.shape[0] // LANES
    for k in range(tiles):
        y_ref[step * tiles + k] = jnp.transpose(y[k * LANES : (k + 1) * LANES])

    @pl.when(step == 0)
    def _():
        mr_ref[...] = mag_ref[...] * jnp.cos(phase_ref[...])
        mi_ref[...] = mag_ref[...] * jnp.sin(phase_ref[...])

    @pl.when(step == pl.num_programs(0) - 1)
    def _():
        group = 2 * channels
        low = lax.broadcasted_iota(jnp.int32, (group, LANES), 1) < owned

        def part(tap, tile):
            return y_ref[tile, tap * group : (tap + 1) * group, :]

        turned = pltpu.roll(part(1, 0) + part(3, 1), owned, 1)
        for j in range(pairs):
            following = pltpu.roll(part(1, j + 1) + part(3, j + 2), owned, 1)
            total = part(0, j) + part(2, j + 1) + jnp.where(low, turned, following)
            f_ref[pl.ds(j, group, stride=pairs), :] = total
            turned = following
        for r in range(2):
            for c in range(channels):
                start = (r * channels + c) * pairs
                msg_ref[c, r] = f_ref[start : start + pairs, :].astype(jnp.bfloat16)


def exchange(
    msg_ref, mag_ref, mr_ref, mi_ref, right_ref, own_ref, gain_ref,
    slots, dense, yr_ref, yi_ref, wr_ref, wi_ref, gr_ref, gi_ref, pack, landed,
    send_sem, recv_sem, fsend_sem, frecv_sem, gsend_sem, grecv_sem, local_sem,
):
    groups = lax.axis_size("gx")
    g = lax.axis_index("gx")
    b = lax.axis_index("bl")
    other = 1 - b
    mesh_id = pl.DeviceIdType.MESH
    pairs = msg_ref.shape[2]
    spectra = 2 * pairs
    tiles = dense.shape[0]
    owned = LANES // 2

    pl.semaphore_wait(pltpu.get_barrier_semaphore(), groups)

    def spread(k, source):
        peer = lax.rem(g + k, groups)
        return pltpu.make_async_remote_copy(
            src_ref=msg_ref.at[peer], dst_ref=slots.at[b, source],
            send_sem=send_sem.at[k], recv_sem=recv_sem.at[k],
            device_id=(peer, b), device_id_type=mesh_id,
        )

    def relay(k, side):
        source = lax.rem(g + groups - k, groups)
        return pltpu.make_async_remote_copy(
            src_ref=slots.at[b, source], dst_ref=slots.at[side, source],
            send_sem=fsend_sem.at[k], recv_sem=frecv_sem.at[k],
            device_id=(g, other), device_id_type=mesh_id,
        )

    def start_spread(k, carry):
        spread(k, g).start()
        return carry

    lax.fori_loop(1, groups, start_spread, 0)
    mine = pltpu.make_async_copy(msg_ref.at[g], slots.at[b, g], local_sem)
    mine.start()
    mine.wait()
    relay(0, b).start()

    def pass_on(k, carry):
        spread(k, lax.rem(g + groups - k, groups)).wait_recv()
        relay(k, b).start()
        return carry

    lax.fori_loop(1, groups, pass_on, 0)

    def collect(k, carry):
        relay(k, other).wait_recv()
        return carry

    lax.fori_loop(0, groups, collect, 0)

    low = lax.broadcasted_iota(jnp.int32, (pairs, LANES), 1) < owned
    for side in range(2):
        for t in range(groups // 2):
            tile = side * (groups // 2) + t
            for r in range(2):
                first = slots[side, 2 * t, r].astype(jnp.float32)
                second = slots[side, 2 * t + 1, r].astype(jnp.float32)
                even = jnp.where(low, first, pltpu.roll(second, owned, 1))
                odd = jnp.where(low, pltpu.roll(first, owned, 1), second)
                both = jnp.concatenate([even, odd], axis=0)
                dense[tile, r * spectra : (r + 1) * spectra, :] = both
                right_ref[
                    r * spectra : (r + 1) * spectra, tile * LANES : (tile + 1) * LANES
                ] = both.astype(jnp.bfloat16)
            diagonal = jnp.sum(dense[tile] * dense[tile], axis=0, keepdims=True)
            wr_ref[tile : tile + 1, :] = diagonal
    for t in range(groups // 2):
        own_ref[t] = dense[b * (groups // 2) + t]

    scale = 1.0 / spectra
    diagonal = wr_ref[...] * scale
    model_real = mr_ref[...]
    model_imag = mi_ref[...]
    magnitude = mag_ref[...]
    inverse_square = 1.0 / (magnitude * magnitude)

    def single_step(gain_real, gain_imag):
        probe_real = gain_real * model_real - gain_imag * model_imag
        probe_imag = gain_real * model_imag + gain_imag * model_real
        yr_ref[...] = probe_real
        yi_ref[...] = probe_imag
        total_real = jnp.zeros((spectra, LANES), jnp.float32)
        total_imag = jnp.zeros((spectra, LANES), jnp.float32)
        for t in range(tiles):
            re = dense[t, :spectra, :]
            im = dense[t, spectra:, :]
            yr = yr_ref[t : t + 1, :]
            yi = yi_ref[t : t + 1, :]
            total_real = total_real + (re * yr + im * yi)
            total_imag = total_imag + (re * yi - im * yr)
        inner_real = jnp.sum(total_real, axis=1, keepdims=True) * scale
        inner_imag = jnp.sum(total_imag, axis=1, keepdims=True) * scale
        inner_real = jnp.broadcast_to(inner_real, (spectra, LANES))
        inner_imag = jnp.broadcast_to(inner_imag, (spectra, LANES))
        for t in range(tiles):
            re = dense[t, :spectra, :]
            im = dense[t, spectra:, :]
            wr_ref[t : t + 1, :] = jnp.sum(
                re * inner_real - im * inner_imag, axis=0, keepdims=True
            )
            wi_ref[t : t + 1, :] = jnp.sum(
                re * inner_imag + im * inner_real, axis=0, keepdims=True
            )
        image_real = wr_ref[...] - diagonal * probe_real
        image_imag = wi_ref[...] - diagonal * probe_imag
        energy = jnp.sum(
            jnp.sum(probe_real * probe_real + probe_imag * probe_imag, axis=1, keepdims=True),
            axis=0,
            keepdims=True,
        ) + epsilon
        factor = inverse_square / energy
        fresh_real = (image_real * model_real + image_imag * model_imag) * factor
        fresh_imag = (image_imag * model_real - image_real * model_imag) * factor
        return (fresh_real, fresh_imag)

    def double_step(pair_index, current):
        first_real, first_imag = single_step(current[0], current[1])
        fresh_real, fresh_imag = single_step(first_real, first_imag)
        return ((fresh_real + first_real) * 0.5, (fresh_imag + first_imag) * 0.5)

    gain_real, gain_imag = lax.fori_loop(
        0,
        ITERS // 2,
        double_step,
        (jnp.ones((tiles, LANES), jnp.float32), jnp.zeros((tiles, LANES), jnp.float32)),
    )
    gr_ref[...] = gain_real
    gi_ref[...] = gain_imag
    half = groups // 2
    own_real = gr_ref[pl.ds(pl.multiple_of(b * half, half), half), :]
    own_imag = gi_ref[pl.ds(pl.multiple_of(b * half, half), half), :]
    low = lax.broadcasted_iota(jnp.int32, (half, LANES), 1) < owned
    even = jnp.where(low, own_real, pltpu.roll(own_imag, owned, 1))
    odd = jnp.where(low, pltpu.roll(own_real, owned, 1), own_imag)
    for t in range(half):
        pack[2 * t] = even[t : t + 1, :]
        pack[2 * t + 1] = odd[t : t + 1, :]

    def hand_back(k, owner):
        peer = lax.rem(g + k, groups)
        return pltpu.make_async_remote_copy(
            src_ref=pack.at[peer], dst_ref=landed.at[owner],
            send_sem=gsend_sem.at[k], recv_sem=grecv_sem.at[k],
            device_id=(peer, b), device_id_type=mesh_id,
        )

    def start_back(k, carry):
        hand_back(k, g).start()
        return carry

    lax.fori_loop(1, groups, start_back, 0)
    landed[g] = pack[g]

    def drain(k, carry):
        spread(k, g).wait_send()
        relay(k, b).wait_send()
        hand_back(k, g).wait_send()
        hand_back(k, lax.rem(g + groups - k, groups)).wait_recv()
        return carry

    relay(0, b).wait_send()
    lax.fori_loop(1, groups, drain, 0)
    for c in range(groups):
        gain_ref[c : c + 1, :] = landed[c]


def greet_all():
    groups = lax.axis_size("gx")
    g = lax.axis_index("gx")
    b = lax.axis_index("bl")
    other = 1 - b
    mesh_id = pl.DeviceIdType.MESH
    barrier = pltpu.get_barrier_semaphore()

    def greet(k, carry):
        pl.semaphore_signal(
            barrier, inc=1, device_id=(lax.rem(g + k, groups), b), device_id_type=mesh_id
        )
        return carry

    lax.fori_loop(1, groups, greet, 0)
    pl.semaphore_signal(barrier, inc=1, device_id=(g, other), device_id_type=mesh_id)


def fused(
    v_ref, bank_ref, mag_ref, phase_ref, right_ref, own_ref, gain_ref,
    msg_ref, mr_ref, mi_ref, y_ref, f_ref, *rest
):
    @pl.when(pl.program_id(0) == 0)
    def _():
        greet_all()

    channelize(v_ref, bank_ref, mag_ref, phase_ref, msg_ref, mr_ref, mi_ref, y_ref, f_ref)

    @pl.when(pl.program_id(0) == pl.num_programs(0) - 1)
    def _():
        exchange(msg_ref, mag_ref, mr_ref, mi_ref, right_ref, own_ref, gain_ref, *rest)


def correlate(own_ref, right_ref, gain_ref, out_ref, owned_ref, real_side, imag_side):
    depth = right_ref.shape[0]
    spectra = depth // 2

    @pl.when(pl.program_id(0) == 0)
    def _():
        real_side[:depth, :] = right_ref[...]
        real_side[depth:, :] = jnp.zeros_like(right_ref)
        imag_side[:depth, :] = jnp.zeros_like(right_ref)
        imag_side[depth:, :] = right_ref[...]
        owned = owned_ref.shape[3]
        owned_ref[0, 0] = gain_ref[:, :owned]
        owned_ref[1, 0] = gain_ref[:, owned:]

    parts = []
    for t in range(own_ref.shape[0]):
        own = own_ref[t] * (1.0 / spectra)
        part = jnp.concatenate([own, own[spectra:], -own[:spectra]], axis=0)
        parts.append(jnp.transpose(part).astype(jnp.bfloat16))
    left = jnp.concatenate(parts, axis=0)
    out_ref[0, 0] = jnp.dot(
        left, real_side[...], preferred_element_type=jnp.float32
    ).astype(jnp.bfloat16)
    out_ref[0, 1] = jnp.dot(
        left, imag_side[...], preferred_element_type=jnp.float32
    ).astype(jnp.bfloat16)


def on_device_tiled(voltages, model_magnitude, model_phase):
    groups = lax.axis_size("gx")
    inputs = model_magnitude.shape[1]
    owned = voltages.shape[1]
    frames_total = voltages.shape[2] // NFFT
    spectra = frames_total - TAPS + 1
    pairs = spectra // 2
    per_step = 4 * LANES // owned
    steps = -(-frames_total // per_step)
    tiles = inputs // LANES
    half = tiles // 2
    bank = jnp.asarray(filter_bank(groups, NFFT // 2 // groups))
    magnitude = model_magnitude.reshape(tiles, LANES)
    phase = model_phase.reshape(tiles, LANES)
    f32 = jnp.float32
    whole = lambda i: (0, 0)
    table = jax.ShapeDtypeStruct((tiles, LANES), f32)
    table_spec = pl.BlockSpec((tiles, LANES), whole)
    right, own, gains = pl.pallas_call(
        fused,
        grid=(steps,),
        in_specs=[
            pl.BlockSpec((1, owned, per_step * NFFT), lambda i: (0, 0, i)),
            pl.BlockSpec(bank.shape, whole),
            table_spec,
            table_spec,
        ],
        out_specs=[
            pl.BlockSpec((2 * spectra, inputs), whole),
            pl.BlockSpec((half, 2 * spectra, LANES), lambda i: (0, 0, 0)),
            pl.BlockSpec((groups, LANES), whole),
        ],
        out_shape=[
            jax.ShapeDtypeStruct((2 * spectra, inputs), jnp.bfloat16),
            jax.ShapeDtypeStruct((half, 2 * spectra, LANES), f32),
            jax.ShapeDtypeStruct((groups, LANES), f32),
        ],
        scratch_shapes=[
            pltpu.VMEM((groups, 2, pairs, LANES), jnp.bfloat16),
            pltpu.VMEM((tiles, LANES), f32),
            pltpu.VMEM((tiles, LANES), f32),
            pltpu.VMEM((steps * 4, TAPS * 2 * groups, LANES), f32),
            pltpu.VMEM((2 * groups * pairs, LANES), f32),
            pltpu.VMEM((2, groups, 2, pairs, LANES), jnp.bfloat16),
            pltpu.VMEM((tiles, 2 * spectra, LANES), f32),
        ]
        + [pltpu.VMEM((tiles, LANES), f32)] * 6
        + [pltpu.VMEM((groups, 1, LANES), f32)] * 2
        + [pltpu.SemaphoreType.DMA((groups,))] * 6
        + [pltpu.SemaphoreType.DMA],
        compiler_params=pltpu.CompilerParams(
            dimension_semantics=("arbitrary",), collective_id=0, has_side_effects=True
        ),
        name="gather_solve",
    )(voltages, bank, magnitude, phase)
    batch = math.gcd(half, 4)
    visibilities, gains = pl.pallas_call(
        correlate,
        grid=(half // batch,),
        in_specs=[
            pl.BlockSpec((batch, 2 * spectra, LANES), lambda i: (i, 0, 0)),
            pl.BlockSpec((2 * spectra, inputs), whole),
            pl.BlockSpec((groups, LANES), whole),
        ],
        out_specs=[
            pl.BlockSpec((1, 2, batch * LANES, inputs), lambda i: (0, 0, i, 0)),
            pl.BlockSpec((2, 1, groups, owned), lambda i: (0, 0, 0, 0)),
        ],
        out_shape=[
            jax.ShapeDtypeStruct((1, 2, half * LANES, inputs), jnp.bfloat16),
            jax.ShapeDtypeStruct((2, 1, groups, owned), f32),
        ],
        scratch_shapes=[pltpu.VMEM((4 * spectra, inputs), jnp.bfloat16)] * 2,
        compiler_params=pltpu.CompilerParams(dimension_semantics=("arbitrary",)),
        name="correlate",
    )(own, right, gains)
    return (visibilities, jnp.swapaxes(gains, 2, 3))


def solution(mesh):
    in_specs = (P("bl", "gx", None), P("gx", None), P("gx", None))
    out_specs = (P("gx", None, "bl", None), P(None, "bl", "gx", None))

    def body(voltages, model_magnitude, model_phase):
        spectra = voltages.shape[2] // NFFT - TAPS + 1
        groups = mesh.shape["gx"]
        tiled = (
            model_magnitude.shape[0] == 1
            and 2 * voltages.shape[1] == LANES
            and mesh.shape["bl"] == 2
            and groups % 16 == 0
            and spectra % 32 == 0
            and spectra & (spectra - 1) == 0
        )
        run = on_device_tiled if tiled else on_device
        return run(voltages, model_magnitude, model_phase)

    return jax.shard_map(
        body, mesh=mesh, in_specs=in_specs, out_specs=out_specs, check_vma=False
    )
```
